128 devices in a mesh: gx: 16 (over x, z_hi, core), gy: 8 (over z_lo, y).
Axes of the slice: x: 4, y: 4, z: 4 (z_hi: 2, z_lo: 2; z = z_hi * 2 + z_lo), core: 2. Of those that a mesh axis runs over, the one named last changes fastest.
Arguments:
- e_field: float32 [3, 24, 256, 2048], P(None, None, 'gx', 'gy'), may hold values from -6 to 6
- h_field: float32 [3, 24, 256, 2048], P(None, None, 'gx', 'gy'), may hold values from -6 to 6
- target: float32 [3, 24, 256, 2048], P(None, None, 'gx', 'gy'), may hold values from -6 to 6
- density: float32 [384, 32768], P('gx', 'gy'), may hold values from 0 to 1
- region_list: int32 [384, 8], P(None, 'gy'), may hold values from 0 to 383, as said below
- source_cells: int32 [3, 512], replicated, may hold values from 0 to 2047, as said below
- source_amp: float32 [2, 3, 512], replicated, may hold values from -6 to 6
Outputs:
- e_final: float32 [3, 24, 256, 2048], P(None, None, 'gx', 'gy')
- h_final: float32 [3, 24, 256, 2048], P(None, None, 'gx', 'gy')
- grad_density: float32 [384, 32768], P('gx', 'gy')
The draws below stay inside these ranges and needn't reach their ends.
Inputs may be any that keep to these rules, and one draw needn't show every extreme that they name: `region_list`: column j lists, for the 24 rows of each optimizer shard along gx in turn, region ids t * 24 + k (plane k of the tile at gx index t in column j); each column holds every id once. One shard holds at most 3 rows of one tile, exactly 3 for some pairs in every column. `source_cells`: row 0 holds planes below 24, row 1 cells along x below 256, row 2 cells along y below 2048; cells may repeat.
All inputs are finite; a program needn't handle non-finite values.
Results may differ from the reference program's by a relative error of at most 0.00002.
Values sent between devices are 32-bit elements; how exact they have to be, the bound alone decides.
A program may use at most 576 MiB of HBM per device.

```python
import jax
import jax.numpy as jnp
import numpy as np
from jax import lax

CX = 16
CY = 256
NZ = 24
NSRC = 512
STEPS = 2
NX = 256
NY = 2048
ROWS = 384
N_GX = 16
N_GY = 8


def column_ids(subkey):
    extra_rows = NZ - N_GX
    pattern = np.array([3] * (extra_rows // 2) + [2] * (extra_rows % 2) + [1] * (N_GX - extra_rows // 2 - extra_rows % 2), dtype=np.int32)
    subkeys = jax.random.split(subkey, 3)
    multiples = jnp.asarray(pattern)[jax.random.permutation(subkeys[0], N_GX)]
    bounds = jnp.cumsum(multiples)
    places = jnp.arange(NZ, dtype=jnp.int32)
    offsets = jnp.sum((bounds[None, :] <= places[:, None]).astype(jnp.int32), axis=1)
    orders = jax.vmap(lambda inner_key: jax.random.permutation(inner_key, NZ))(jax.random.split(subkeys[1], N_GX))
    shards = jnp.arange(N_GX, dtype=jnp.int32)
    tile_of = (shards[:, None] + offsets[None, :]) % N_GX
    planes = orders[tile_of, places[None, :]]
    region_ids = tile_of * NZ + planes
    shuffle = jax.vmap(lambda inner_key: jax.random.permutation(inner_key, NZ))(jax.random.split(subkeys[2], N_GX))
    region_ids = jnp.take_along_axis(region_ids, shuffle, axis=1)
    return region_ids.reshape(N_GX * NZ).astype(jnp.int32)


def draw_region_list(key, part):
    columns = [column_ids(jax.random.fold_in(key, 7000 + column)) for column in range(N_GY)]
    return jnp.stack(columns, axis=1).astype(jnp.int32)


def draw_source_cells(key, part):
    subkeys = jax.random.split(jax.random.fold_in(key, 91), 3)
    planes = jax.random.randint(subkeys[0], (NSRC,), 0, NZ)
    across = jax.random.randint(subkeys[1], (NSRC,), 0, NX)
    lateral = jax.random.randint(subkeys[2], (NSRC,), 0, NY)
    across = across.at[0].set(NX - 1).at[1].set(0)
    lateral = lateral.at[0].set(NY - 1)
    return jnp.stack([planes, across, lateral]).astype(jnp.int32)


def steps_of(own_key, extent, cuts, low, high):
    def one(dim, blocks):
        steps = jax.random.uniform(jax.random.fold_in(jax.random.fold_in(own_key, 6), dim), (blocks,), jnp.float32, low / len(cuts), high / len(cuts))
        return jnp.repeat(jnp.exp(steps), extent[dim] // blocks).reshape((-1,) + (1,) * (len(extent) - dim - 1))

    level = one(*cuts[0])
    for cut in cuts[1:]:
        level = level * one(*cut)
    return level


def scatter_about(key, dims, deviation, bound, cuts=(), kind=jnp.bfloat16):
    result = jax.random.normal(key, dims, jnp.float32) * deviation
    if len(cuts) > 0:
        result = steps_of(key, dims, cuts, -0.22, 0.18) * result
    return jnp.clip(result, min=-bound, max=bound).astype(kind)


def setup_inputs(seed: int = 0) -> dict:
    seeds = jax.random.split(jax.random.key(seed), 8)
    return {
        "e_field": scatter_about(seeds[0], (3, NZ, NX, NY), 1.0, 6.0, ((2, 16), (3, 8)), jnp.float32),
        "h_field": scatter_about(seeds[1], (3, NZ, NX, NY), 1.0, 6.0, ((2, 16), (3, 8)), jnp.float32),
        "target": scatter_about(seeds[2], (3, NZ, NX, NY), 1.0, 6.0, ((2, 16), (3, 8)), jnp.float32),
        "density": jnp.clip(1.0 * jax.random.uniform(seeds[3], (ROWS, N_GY * CX * CY), jnp.float32) ** steps_of(seeds[3], (ROWS, N_GY * CX * CY), ((0, 16), (1, 8)), -0.2, 0.2), 0.0, 1.0),
        "region_list": draw_region_list(jax.random.fold_in(seeds[7], 71), 0),
        "source_cells": draw_source_cells(jax.random.fold_in(seeds[7], 71), 0),
        "source_amp": scatter_about(seeds[6], (STEPS, 3, NSRC), 1.0, 6.0, (), jnp.float32),
    }


STEP_DT = 0.5
SHARPNESS = 4.0
MIDPOINT = 0.5
EPS_LOW = 1.0
EPS_SPAN = 3.0

def diff_ahead(values, which_axis):
    upper_side = jnp.concatenate([lax.slice_in_dim(values, 1, values.shape[which_axis], axis=which_axis), jnp.zeros_like(lax.slice_in_dim(values, 0, 1, axis=which_axis))], axis=which_axis)
    return upper_side - values

def diff_behind(values, which_axis):
    lower_side = jnp.concatenate([jnp.zeros_like(lax.slice_in_dim(values, 0, 1, axis=which_axis)), lax.slice_in_dim(values, 0, values.shape[which_axis] - 1, axis=which_axis)], axis=which_axis)
    return values - lower_side

def curl_ahead(fields):
    comp_x = diff_ahead(fields[2], 2) - diff_ahead(fields[1], 0)
    comp_y = diff_ahead(fields[0], 0) - diff_ahead(fields[2], 1)
    comp_z = diff_ahead(fields[1], 1) - diff_ahead(fields[0], 2)
    return jnp.stack([comp_x, comp_y, comp_z])

def curl_behind(fields):
    comp_x = diff_behind(fields[2], 2) - diff_behind(fields[1], 0)
    comp_y = diff_behind(fields[0], 0) - diff_behind(fields[2], 1)
    comp_z = diff_behind(fields[1], 1) - diff_behind(fields[0], 2)
    return jnp.stack([comp_x, comp_y, comp_z])

def smooth_rows(planes):
    padded = jnp.pad(planes, ((0, 0), (1, 1), (1, 1)))
    return 0.5 * planes + 0.125 * (padded[:, 2:, 1:-1] + padded[:, :-2, 1:-1] + padded[:, 1:-1, 2:] + padded[:, 1:-1, :-2])

def project(filtered):
    norm_term = 2.0 * jnp.tanh(SHARPNESS * MIDPOINT)
    return (jnp.tanh(SHARPNESS * MIDPOINT) + jnp.tanh(SHARPNESS * (filtered - MIDPOINT))) / norm_term

def project_slope(filtered):
    inner_tanh = jnp.tanh(SHARPNESS * (filtered - MIDPOINT))
    return SHARPNESS * (1.0 - inner_tanh * inner_tanh) / (2.0 * jnp.tanh(SHARPNESS * MIDPOINT))

def reference(e_field, h_field, target, density, region_list, source_cells, source_amp):
    design_rows = density.reshape(N_GX * NZ * N_GY, CX, CY)
    filtered = smooth_rows(design_rows).reshape(N_GX * NZ, N_GY, CX, CY)
    projected = project(filtered)
    tile_of = (region_list // NZ).astype(jnp.int32)
    plane_of = (region_list % NZ).astype(jnp.int32)
    column_of = jnp.broadcast_to(jnp.arange(N_GY, dtype=jnp.int32)[None, :], region_list.shape).astype(jnp.int32)
    grid_blocks = jnp.zeros((NZ, N_GX, CX, N_GY, CY), jnp.float32)
    grid_blocks = grid_blocks.at[plane_of, tile_of, :, column_of, :].set(projected)
    rho_grid = grid_blocks.reshape(NZ, NX, NY)
    source_list = []
    for timestep in range(STEPS):
        source_list.append(jnp.zeros((3, NZ, NX, NY), jnp.float32).at[:, source_cells[0], source_cells[1], source_cells[2]].add(source_amp[timestep]))

    def evolve(rho_values):
        inv_eps = 1.0 / (EPS_LOW + EPS_SPAN * rho_values)
        electric = e_field
        magnetic = h_field
        for timestep in range(STEPS):
            magnetic = magnetic - STEP_DT * curl_ahead(electric)
            curl_now = curl_behind(magnetic)
            electric = electric + STEP_DT * inv_eps[None] * curl_now + STEP_DT * source_list[timestep]
        misfit = electric - target
        return (0.5 * jnp.sum(misfit * misfit), (electric, magnetic))
    loss_value, pullback, finals = jax.vjp(evolve, rho_grid, has_aux=True)
    rho_grad = pullback(jnp.ones_like(loss_value))[0]
    grad_blocks = rho_grad.reshape(NZ, N_GX, CX, N_GY, CY)
    row_grads = grad_blocks[plane_of, tile_of, :, column_of, :] * project_slope(filtered)
    grad_density = smooth_rows(row_grads.reshape(N_GX * NZ * N_GY, CX, CY)).reshape(N_GX * NZ, N_GY * CX * CY)
    return (finals[0], finals[1], grad_density)
```

```python
import jax
import jax.numpy as jnp
from jax import lax
from jax.experimental import pallas as pl
from jax.experimental.pallas import tpu as pltpu
from jax.sharding import PartitionSpec as P

CX = 16
CY = 256
NZ = 24
STEPS = 2
CAP = 3
NSRC = 512
WIDTH = CX * CY

STEP_DT = 0.5
SHARPNESS = 4.0
MIDPOINT = 0.5
EPS_LOW = 1.0
EPS_SPAN = 3.0
TANH_MID = 0.9640275800758169

F32 = jnp.float32
MESH = pl.DeviceIdType.MESH


def index_tables(region_list, n_gx):
    me = lax.axis_index("gx")
    ids = region_list[:, 0].reshape(n_gx, NZ)
    tile, plane = ids // NZ, ids % NZ
    place = jnp.arange(NZ, dtype=jnp.int32)
    earlier = place[None, :] < place[:, None]
    rank = jnp.sum(
        ((tile[:, :, None] == tile[:, None, :]) & earlier[None]).astype(jnp.int32), axis=2
    )
    own_tile = lax.dynamic_slice_in_dim(tile, me, 1)[0]
    own_rank = lax.dynamic_slice_in_dim(rank, me, 1)[0]
    own_slot = own_tile * CAP + own_rank
    slots = jnp.arange(n_gx * CAP, dtype=jnp.int32)
    send_rows = jnp.sum(jnp.where(own_slot[None, :] == slots[:, None], place[None, :], 0), axis=1)
    shard_slot = jnp.arange(n_gx, dtype=jnp.int32)[:, None] * CAP + rank
    shard_slot_here = jnp.where(tile == me, shard_slot, -1)
    send_planes = jnp.sum(
        jnp.where(shard_slot_here[None] == slots[:, None, None], plane[None], 0), axis=(1, 2)
    )
    take_planes = jnp.sum(
        jnp.where(ids[None] == (me * NZ + place)[:, None, None], shard_slot[None], 0), axis=(1, 2)
    )
    return jnp.concatenate([send_rows, send_planes, take_planes, own_slot]).astype(jnp.int32)


def kernel(n_gx, n_gy, idx, cells, amp, e_hbm, h_hbm, t_hbm, d_hbm, e_out, h_out, g_out,
           E, H, T, D, SL, C1, C2, G, S, L, ROW, INV, EG, SEND1, RECV1, SEND2, RECV2,
           XS, XR, YS, YR, local_sem, row_send, row_recv, x_send, x_recv, y_send, y_recv):
    gx = lax.axis_index("gx")
    gy = lax.axis_index("gy")
    n_slots = n_gx * CAP
    row_lines = ROW.reshape(2 * NZ * CX, 128)

    barrier = pltpu.get_barrier_semaphore()
    for d in range(1, n_gx):
        pl.semaphore_signal(barrier, inc=1, device_id=(lax.rem(gx + d, n_gx), gy), device_id_type=MESH)
    for d in (1, n_gy - 1):
        pl.semaphore_signal(barrier, inc=1, device_id=(gx, lax.rem(gy + d, n_gy)), device_id_type=MESH)

    load_d = pltpu.make_async_copy(d_hbm, D.at[:, CY:CY + WIDTH], local_sem.at[0])
    load_e = pltpu.make_async_copy(e_hbm, E.at[:, 0:NZ], local_sem.at[1])
    load_h = pltpu.make_async_copy(h_hbm, H.at[:, 1:NZ + 1], local_sem.at[2])
    load_t = pltpu.make_async_copy(t_hbm, T, local_sem.at[3])
    load_d.start()
    load_e.start()
    load_h.start()
    load_t.start()

    zero_plane = jnp.zeros((CX, CY), F32)
    for c in range(3):
        E[c, NZ] = zero_plane
        G[c, NZ] = zero_plane
        H[c, 0] = zero_plane
    D[:, 0:CY] = jnp.zeros((NZ, CY), F32)
    D[:, CY + WIDTH:] = jnp.zeros((NZ, CY), F32)

    lane_wide = lax.broadcasted_iota(jnp.int32, (NZ, CY), 1)
    sub = lax.broadcasted_iota(jnp.int32, (CX, CY), 0)
    lane128 = lax.broadcasted_iota(jnp.int32, (CX, 128), 1)
    first_row, last_row = sub == 0, sub == CX - 1
    first_lane, last_lane = lane128 == 0, lane128 == 127
    wide_first, wide_last = lane_wide == 0, lane_wide == CY - 1

    def smooth(ref, a):
        at = pl.multiple_of((a + 1) * CY, CY)
        mid = ref[:, pl.ds(at, CY)]
        low = ref[:, pl.ds(pl.multiple_of(at - CY, CY), CY)]
        high = ref[:, pl.ds(pl.multiple_of(at + CY, CY), CY)]
        right = jnp.where(wide_last, 0.0, pltpu.roll(mid, CY - 1, 1))
        left = jnp.where(wide_first, 0.0, pltpu.roll(mid, 1, 1))
        return 0.5 * mid + 0.125 * (high + low + right + left)

    load_d.wait()

    def rows_in(a, carry):
        filtered = smooth(D, a)
        inner = jnp.tanh(SHARPNESS * (filtered - MIDPOINT))
        SL[:, pl.ds(pl.multiple_of(a * CY, CY), CY)] = (
            SHARPNESS * (1.0 - inner * inner) / (2.0 * TANH_MID)
        )
        projected = (TANH_MID + inner) / (2.0 * TANH_MID)
        for half in range(2):
            row_lines[pl.ds(half * NZ * CX + a, NZ, stride=CX), :] = projected[:, half * 128:half * 128 + 128]
        return carry

    lax.fori_loop(0, CX, rows_in, 0)

    def pack_rows(slot, carry):
        row = idx[slot]
        SEND1[slot, :, 0:128] = ROW[row]
        SEND1[slot, :, 128:256] = ROW[NZ + row]
        return carry

    lax.fori_loop(0, n_slots, pack_rows, 0)

    def pack_low(acc, z, k, fx, fy, fz):
        XS[k, pl.ds(z, 1), :] = fy[0:1, :]
        XS[k, pl.ds(NZ + z, 1), :] = fz[0:1, :]
        acc = jnp.where(lane128 == z, pltpu.roll(fx[:, 0:128], z, 1), acc)
        return jnp.where(lane128 == NZ + z, pltpu.roll(fz[:, 0:128], NZ + z, 1), acc)

    def pack_high(acc, z, k, fx, fy, fz):
        XS[k, pl.ds(z, 1), :] = fy[CX - 1:CX, :]
        XS[k, pl.ds(NZ + z, 1), :] = fz[CX - 1:CX, :]
        acc = jnp.where(lane128 == z, pltpu.roll(fx[:, 128:256], z + 1, 1), acc)
        return jnp.where(lane128 == NZ + z, pltpu.roll(fz[:, 128:256], NZ + z + 1, 1), acc)

    def rim_copies(k, down):
        step_x = n_gx - 1 if down else 1
        step_y = n_gy - 1 if down else 1
        across = pltpu.make_async_remote_copy(
            src_ref=XS.at[k], dst_ref=XR.at[k], send_sem=x_send.at[k], recv_sem=x_recv.at[k],
            device_id=(lax.rem(gx + step_x, n_gx), gy), device_id_type=MESH)
        lateral = pltpu.make_async_remote_copy(
            src_ref=YS.at[k], dst_ref=YR.at[k], send_sem=y_send.at[k], recv_sem=y_recv.at[k],
            device_id=(gx, lax.rem(gy + step_y, n_gy)), device_id_type=MESH)
        return across, lateral

    def start_rims(k, down):
        across, lateral = rim_copies(k, down)
        across.start()
        lateral.start()

    def finish_rims(k, down):
        across, lateral = rim_copies(k, down)
        across.wait()
        lateral.wait()
        edge_x = gx == (n_gx - 1 if down else 0)
        edge_y = gy == (n_gy - 1 if down else 0)
        XR[k] = XR[k] * jnp.where(edge_x, 0.0, 1.0)
        YR[k] = YR[k] * jnp.where(edge_y, 0.0, 1.0)

    blank = jnp.zeros((CX, 128), F32)

    def curl_ahead(F, z, k):
        fx, fy, fz = F[0, z], F[1, z], F[2, z]
        rim_y = XR[k, pl.ds(z, 1), :]
        rim_z = XR[k, pl.ds(NZ + z, 1), :]
        lat = YR[k]
        lat_x = pltpu.roll(lat, 127 - z, 1)
        lat_z = pltpu.roll(lat, 127 - NZ - z, 1)

        def up_x(v, rim):
            return jnp.where(last_row, rim, pltpu.roll(v, CX - 1, 0))

        def up_y(v, lateral):
            r = pltpu.roll(v, CY - 1, 1)
            return jnp.concatenate([r[:, 0:128], jnp.where(last_lane, lateral, r[:, 128:256])], axis=1)

        cx = (up_y(fz, lat_z) - fz) - (F[1, z + 1] - fy)
        cy = (F[0, z + 1] - fx) - (up_x(fz, rim_z) - fz)
        cz = (up_x(fy, rim_y) - fy) - (up_y(fx, lat_x) - fx)
        return cx, cy, cz

    def curl_behind(F, z, k):
        fx, fy, fz = F[0, z + 1], F[1, z + 1], F[2, z + 1]
        rim_y = XR[k, pl.ds(z, 1), :]
        rim_z = XR[k, pl.ds(NZ + z, 1), :]
        lat = YR[k]
        lat_x = pltpu.roll(lat, lax.rem(128 - z, 128), 1)
        lat_z = pltpu.roll(lat, 128 - NZ - z, 1)

        def dn_x(v, rim):
            return jnp.where(first_row, rim, pltpu.roll(v, 1, 0))

        def dn_y(v, lateral):
            r = pltpu.roll(v, 1, 1)
            return jnp.concatenate([jnp.where(first_lane, lateral, r[:, 0:128]), r[:, 128:256]], axis=1)

        cx = (fz - dn_y(fz, lat_z)) - (fy - F[1, z])
        cy = (fx - F[0, z]) - (fz - dn_x(fz, rim_z))
        cz = (fy - dn_x(fy, rim_y)) - (fx - dn_y(fx, lat_x))
        return cx, cy, cz

    load_e.wait()

    def pack_e0(z, acc):
        return pack_low(acc, z, 0, E[0, z], E[1, z], E[2, z])

    YS[0] = lax.fori_loop(0, NZ, pack_e0, blank)

    pl.semaphore_wait(barrier, n_gx + 1)
    start_rims(0, True)

    def row_copy(send, recv, d, which):
        peer = lax.rem(gx + d, n_gx)
        return pltpu.make_async_remote_copy(
            src_ref=send.at[pl.ds(peer * CAP, CAP)], dst_ref=recv.at[pl.ds(gx * CAP, CAP)],
            send_sem=row_send.at[which, d], recv_sem=row_recv.at[which, d],
            device_id=(peer, gy), device_id_type=MESH)

    for d in range(1, n_gx):
        row_copy(SEND1, RECV1, d, 0).start()
    for s in range(CAP):
        RECV1[gx * CAP + s] = SEND1[gx * CAP + s]

    load_h.wait()
    finish_rims(0, True)

    def h_first(z, acc):
        cx, cy, cz = curl_ahead(E, z, 0)
        hx = H[0, z + 1] - STEP_DT * cx
        hy = H[1, z + 1] - STEP_DT * cy
        hz = H[2, z + 1] - STEP_DT * cz
        H[0, z + 1] = hx
        H[1, z + 1] = hy
        H[2, z + 1] = hz
        return pack_high(acc, z, 1, hx, hy, hz)

    YS[1] = lax.fori_loop(0, NZ, h_first, blank)
    start_rims(1, False)

    local_x = cells[1:2, :] - gx * CX
    inside = (local_x >= 0) & (local_x < CX)
    where_zx = jnp.where(inside, cells[0:1, :] * CX + local_x, -1)
    where_y = cells[2:3, :] - gy * CY
    sub_src = lax.broadcasted_iota(jnp.int32, (CX, NSRC), 0)

    def build_hits(z, carry):
        hit = sub_src == where_zx - z * CX
        L[pl.ds(pl.multiple_of(z * CX, CX), CX), :] = jnp.where(hit, 1.0, 0.0).astype(jnp.bfloat16)
        return carry

    lax.fori_loop(0, NZ, build_hits, 0)
    hit_y = lax.broadcasted_iota(jnp.int32, (CY, NSRC), 0) == where_y

    for n in range(STEPS):
        for c in range(3):
            row = amp[n, c:c + 1, :]
            high = row.astype(jnp.bfloat16).astype(F32)
            rest = row - high
            mid = rest.astype(jnp.bfloat16).astype(F32)
            low = rest - mid
            total = None
            for part in (high, mid, low):
                cols = jnp.where(hit_y, part, 0.0).astype(jnp.bfloat16)
                term = lax.dot_general(L[...], cols, (((1,), (1,)), ((), ())),
                                       preferred_element_type=F32)
                total = term if total is None else total + term
            S[n * 3 + c] = total.reshape(NZ, CX, CY)

    finish_rims(1, False)

    def c_first(z, carry):
        cx, cy, cz = curl_behind(H, z, 1)
        C1[0, z] = cx
        C1[1, z] = cy
        C1[2, z] = cz
        return carry

    lax.fori_loop(0, NZ, c_first, 0)

    for d in range(1, n_gx):
        row_copy(SEND1, RECV1, d, 0).wait()

    def e_first(z, acc):
        inv = 1.0 / (EPS_LOW + EPS_SPAN * RECV1[idx[2 * n_slots + z]])
        INV[z] = inv
        new = []
        for c in range(3):
            value = E[c, z] + STEP_DT * inv * C1[c, z] + STEP_DT * S[c, z]
            E[c, z] = value
            new.append(value)
        return pack_low(acc, z, 2, *new)

    YS[2] = lax.fori_loop(0, NZ, e_first, blank)
    start_rims(2, True)
    finish_rims(2, True)

    def h_second(z, acc):
        curls = curl_ahead(E, z, 2)
        new = []
        for c in range(3):
            value = H[c, z + 1] - STEP_DT * curls[c]
            H[c, z + 1] = value
            new.append(value)
        return pack_high(acc, z, 3, *new)

    YS[3] = lax.fori_loop(0, NZ, h_second, blank)
    start_rims(3, False)
    save_h = pltpu.make_async_copy(H.at[:, 1:NZ + 1], h_out, local_sem.at[4])
    save_h.start()
    load_t.wait()
    finish_rims(3, False)

    def e_second(z, acc):
        curls = curl_behind(H, z, 3)
        inv = INV[z]
        half_inv = STEP_DT * inv
        grad = None
        new = []
        for c in range(3):
            value = E[c, z] + half_inv * curls[c] + STEP_DT * S[3 + c, z]
            E[c, z] = value
            misfit = value - T[c, z]
            T[c, z] = misfit
            grad = curls[c] * misfit if grad is None else grad + curls[c] * misfit
            value = half_inv * misfit
            G[c, z] = value
            new.append(value)
        EG[z] = grad
        return pack_low(acc, z, 4, *new)

    YS[4] = lax.fori_loop(0, NZ, e_second, blank)
    start_rims(4, True)
    save_e = pltpu.make_async_copy(E.at[:, 0:NZ], e_out, local_sem.at[5])
    save_e.start()
    finish_rims(4, True)

    for c in range(3):
        C2[c, 0] = zero_plane

    def adjoint_h(z, acc):
        curls = curl_ahead(G, z, 4)
        for c in range(3):
            C2[c, z + 1] = curls[c]
        return pack_high(acc, z, 5, *curls)

    YS[5] = lax.fori_loop(0, NZ, adjoint_h, blank)
    start_rims(5, False)
    finish_rims(5, False)

    def adjoint_e(z, carry):
        curls = curl_behind(C2, z, 5)
        grad = EG[z]
        for c in range(3):
            grad = grad + C1[c, z] * (T[c, z] - STEP_DT * curls[c])
        inv = INV[z]
        EG[z] = (-EPS_SPAN * STEP_DT) * (inv * inv) * grad
        return carry

    lax.fori_loop(0, NZ, adjoint_e, 0)

    def pack_planes(slot, carry):
        SEND2[slot] = EG[idx[n_slots + slot]]
        return carry

    lax.fori_loop(0, n_slots, pack_planes, 0)
    for d in range(1, n_gx):
        row_copy(SEND2, RECV2, d, 1).start()
    for s in range(CAP):
        RECV2[gx * CAP + s] = SEND2[gx * CAP + s]
    for d in range(1, n_gx):
        row_copy(SEND2, RECV2, d, 1).wait()

    def unpack(r, carry):
        plane = RECV2[idx[2 * n_slots + NZ + r]]
        ROW[r] = plane[:, 0:128]
        ROW[NZ + r] = plane[:, 128:256]
        return carry

    lax.fori_loop(0, NZ, unpack, 0)

    def scale(a, carry):
        own = SL[:, pl.ds(pl.multiple_of(a * CY, CY), CY)]
        parts = [row_lines[pl.ds(half * NZ * CX + a, NZ, stride=CX), :] for half in range(2)]
        D[:, pl.ds(pl.multiple_of((a + 1) * CY, CY), CY)] = jnp.concatenate(parts, axis=1) * own
        return carry

    lax.fori_loop(0, CX, scale, 0)

    def rows_out(a, carry):
        SL[:, pl.ds(pl.multiple_of(a * CY, CY), CY)] = smooth(D, a)
        return carry

    lax.fori_loop(0, CX, rows_out, 0)
    save_g = pltpu.make_async_copy(SL, g_out, local_sem.at[6])
    save_g.start()
    save_h.wait()
    save_e.wait()
    save_g.wait()


def solution(mesh):
    n_gx, n_gy = mesh.shape["gx"], mesh.shape["gy"]
    n_slots = n_gx * CAP
    placed = (
        P(None, None, "gx", "gy"),
        P(None, None, "gx", "gy"),
        P(None, None, "gx", "gy"),
        P("gx", "gy"),
        P(None, "gy"),
        P(),
        P(),
    )
    field = (3, NZ, CX, CY)
    padded = (3, NZ + 1, CX, CY)

    def body(e_field, h_field, target, density, region_list, source_cells, source_amp):
        idx = index_tables(region_list, n_gx)
        any_spec = pl.BlockSpec(memory_space=pl.ANY)
        vmem = pl.BlockSpec(memory_space=pltpu.VMEM)
        smem = pl.BlockSpec(memory_space=pltpu.SMEM)

        def run(*refs):
            kernel(n_gx, n_gy, *refs)

        dma = pltpu.SemaphoreType.DMA
        return pl.pallas_call(
            run,
            name="yee_adjoint",
            out_shape=(
                jax.ShapeDtypeStruct(field, F32),
                jax.ShapeDtypeStruct(field, F32),
                jax.ShapeDtypeStruct((NZ, WIDTH), F32),
            ),
            in_specs=[smem, vmem, vmem, any_spec, any_spec, any_spec, any_spec],
            out_specs=(any_spec, any_spec, any_spec),
            scratch_shapes=[
                pltpu.VMEM(padded, F32),
                pltpu.VMEM(padded, F32),
                pltpu.VMEM(field, F32),
                pltpu.VMEM((NZ, WIDTH + 2 * CY), F32),
                pltpu.VMEM((NZ, WIDTH), F32),
                pltpu.VMEM(field, F32),
                pltpu.VMEM(padded, F32),
                pltpu.VMEM(padded, F32),
                pltpu.VMEM((STEPS * 3, NZ, CX, CY), F32),
                pltpu.VMEM((NZ * CX, NSRC), jnp.bfloat16),
                pltpu.VMEM((2 * NZ, CX, 128), F32),
                pltpu.VMEM((NZ, CX, CY), F32),
                pltpu.VMEM((NZ, CX, CY), F32),
                pltpu.VMEM((n_slots, CX, CY), F32),
                pltpu.VMEM((n_slots, CX, CY), F32),
                pltpu.VMEM((n_slots, CX, CY), F32),
                pltpu.VMEM((n_slots, CX, CY), F32),
                pltpu.VMEM((6, 2 * NZ, CY), F32),
                pltpu.VMEM((6, 2 * NZ, CY), F32),
                pltpu.VMEM((6, CX, 128), F32),
                pltpu.VMEM((6, CX, 128), F32),
                dma((7,)),
                dma((2, n_gx)),
                dma((2, n_gx)),
                dma((6,)),
                dma((6,)),
                dma((6,)),
                dma((6,)),
            ],
            compiler_params=pltpu.CompilerParams(collective_id=0, has_side_effects=True),
        )(idx, source_cells, source_amp, e_field, h_field, target, density)

    return jax.shard_map(
        body,
        mesh=mesh,
        in_specs=placed,
        out_specs=(P(None, None, "gx", "gy"), P(None, None, "gx", "gy"), P("gx", "gy")),
        check_vma=False,
    )
```

```python
import jax
import jax.numpy as jnp
from jax import lax
from jax.experimental import pallas as pl
from jax.experimental.pallas import tpu as pltpu
from jax.sharding import PartitionSpec as P

CX = 16
CY = 256
NZ = 24
STEPS = 2
CAP = 3
NSRC = 512
WIDTH = CX * CY

STEP_DT = 0.5
SHARPNESS = 4.0
MIDPOINT = 0.5
EPS_LOW = 1.0
EPS_SPAN = 3.0
TANH_MID = 0.9640275800758169

F32 = jnp.float32
MESH = pl.DeviceIdType.MESH


def index_tables(region_list, n_gx):
    me = lax.axis_index("gx")
    ids = region_list[:, 0].reshape(n_gx, NZ)
    tile, plane = ids // NZ, ids % NZ
    place = jnp.arange(NZ, dtype=jnp.int32)
    earlier = place[None, :] < place[:, None]
    rank = jnp.sum(
        ((tile[:, :, None] == tile[:, None, :]) & earlier[None]).astype(jnp.int32), axis=2
    )
    own_tile = lax.dynamic_slice_in_dim(tile, me, 1)[0]
    own_rank = lax.dynamic_slice_in_dim(rank, me, 1)[0]
    own_slot = own_tile * CAP + own_rank
    slots = jnp.arange(n_gx * CAP, dtype=jnp.int32)
    send_rows = jnp.sum(jnp.where(own_slot[None, :] == slots[:, None], place[None, :], 0), axis=1)
    shard_slot = jnp.arange(n_gx, dtype=jnp.int32)[:, None] * CAP + rank
    shard_slot_here = jnp.where(tile == me, shard_slot, -1)
    send_planes = jnp.sum(
        jnp.where(shard_slot_here[None] == slots[:, None, None], plane[None], 0), axis=(1, 2)
    )
    take_planes = jnp.sum(
        jnp.where(ids[None] == (me * NZ + place)[:, None, None], shard_slot[None], 0), axis=(1, 2)
    )
    return jnp.concatenate([send_rows, send_planes, take_planes, own_slot]).astype(jnp.int32)


def kernel(n_gx, n_gy, idx, cells, amp, e_hbm, h_hbm, t_hbm, d_hbm, e_out, h_out, g_out,
           E, H, T, D, SL, C1, C2, G, S, L, ROW, INV, EG, SEND1, RECV1, SEND2, RECV2,
           XS, XR, YS, YR, local_sem, row_send, row_recv, x_send, x_recv, y_send, y_recv):
    gx = lax.axis_index("gx")
    gy = lax.axis_index("gy")
    n_slots = n_gx * CAP
    row_lines = ROW.reshape(2 * NZ * CX, 128)

    barrier = pltpu.get_barrier_semaphore()
    for d in range(1, n_gx):
        pl.semaphore_signal(barrier, inc=1, device_id=(lax.rem(gx + d, n_gx), gy), device_id_type=MESH)
    for d in (1, n_gy - 1):
        pl.semaphore_signal(barrier, inc=1, device_id=(gx, lax.rem(gy + d, n_gy)), device_id_type=MESH)

    load_d = pltpu.make_async_copy(d_hbm, D.at[:, CY:CY + WIDTH], local_sem.at[0])
    load_e = pltpu.make_async_copy(e_hbm, E.at[:, 0:NZ], local_sem.at[1])
    load_h = pltpu.make_async_copy(h_hbm, H.at[:, 1:NZ + 1], local_sem.at[2])
    load_t = pltpu.make_async_copy(t_hbm, T, local_sem.at[3])
    load_d.start()
    load_e.start()
    load_h.start()
    load_t.start()

    zero_plane = jnp.zeros((CX, CY), F32)
    for c in range(3):
        E[c, NZ] = zero_plane
        G[c, NZ] = zero_plane
        H[c, 0] = zero_plane
    D[:, 0:CY] = jnp.zeros((NZ, CY), F32)
    D[:, CY + WIDTH:] = jnp.zeros((NZ, CY), F32)

    lane_wide = lax.broadcasted_iota(jnp.int32, (NZ, CY), 1)
    sub = lax.broadcasted_iota(jnp.int32, (CX, CY), 0)
    lane128 = lax.broadcasted_iota(jnp.int32, (CX, 128), 1)
    first_row, last_row = sub == 0, sub == CX - 1
    first_lane, last_lane = lane128 == 0, lane128 == 127
    wide_first, wide_last = lane_wide == 0, lane_wide == CY - 1

    def smooth(ref, a):
        at = pl.multiple_of((a + 1) * CY, CY)
        mid = ref[:, pl.ds(at, CY)]
        low = ref[:, pl.ds(pl.multiple_of(at - CY, CY), CY)]
        high = ref[:, pl.ds(pl.multiple_of(at + CY, CY), CY)]
        right = jnp.where(wide_last, 0.0, pltpu.roll(mid, CY - 1, 1))
        left = jnp.where(wide_first, 0.0, pltpu.roll(mid, 1, 1))
        return 0.5 * mid + 0.125 * (high + low + right + left)

    load_d.wait()

    def rows_in(a, carry):
        filtered = smooth(D, a)
        inner = jnp.tanh(SHARPNESS * (filtered - MIDPOINT))
        SL[:, pl.ds(pl.multiple_of(a * CY, CY), CY)] = (
            SHARPNESS * (1.0 - inner * inner) / (2.0 * TANH_MID)
        )
        projected = (TANH_MID + inner) / (2.0 * TANH_MID)
        for half in range(2):
            row_lines[pl.ds(half * NZ * CX + a, NZ, stride=CX), :] = projected[:, half * 128:half * 128 + 128]
        return carry

    lax.fori_loop(0, CX, rows_in, 0, unroll=CX)

    def pack_rows(slot, carry):
        row = idx[slot]
        SEND1[slot, :, 0:128] = ROW[row]
        SEND1[slot, :, 128:256] = ROW[NZ + row]
        return carry

    lax.fori_loop(0, n_slots, pack_rows, 0, unroll=8)

    def pack_low(acc, z, k, fx, fy, fz):
        XS[k, pl.ds(z, 1), :] = fy[0:1, :]
        XS[k, pl.ds(NZ + z, 1), :] = fz[0:1, :]
        acc = jnp.where(lane128 == z, pltpu.roll(fx[:, 0:128], z, 1), acc)
        return jnp.where(lane128 == NZ + z, pltpu.roll(fz[:, 0:128], NZ + z, 1), acc)

    def pack_high(acc, z, k, fx, fy, fz):
        XS[k, pl.ds(z, 1), :] = fy[CX - 1:CX, :]
        XS[k, pl.ds(NZ + z, 1), :] = fz[CX - 1:CX, :]
        acc = jnp.where(lane128 == z, pltpu.roll(fx[:, 128:256], z + 1, 1), acc)
        return jnp.where(lane128 == NZ + z, pltpu.roll(fz[:, 128:256], NZ + z + 1, 1), acc)

    def rim_copies(k, down):
        step_x = n_gx - 1 if down else 1
        step_y = n_gy - 1 if down else 1
        across = pltpu.make_async_remote_copy(
            src_ref=XS.at[k], dst_ref=XR.at[k], send_sem=x_send.at[k], recv_sem=x_recv.at[k],
            device_id=(lax.rem(gx + step_x, n_gx), gy), device_id_type=MESH)
        lateral = pltpu.make_async_remote_copy(
            src_ref=YS.at[k], dst_ref=YR.at[k], send_sem=y_send.at[k], recv_sem=y_recv.at[k],
            device_id=(gx, lax.rem(gy + step_y, n_gy)), device_id_type=MESH)
        return across, lateral

    def start_rims(k, down):
        across, lateral = rim_copies(k, down)
        across.start()
        lateral.start()

    def finish_rims(k, down):
        across, lateral = rim_copies(k, down)
        across.wait()
        lateral.wait()
        edge_x = gx == (n_gx - 1 if down else 0)
        edge_y = gy == (n_gy - 1 if down else 0)
        XR[k] = XR[k] * jnp.where(edge_x, 0.0, 1.0)
        YR[k] = YR[k] * jnp.where(edge_y, 0.0, 1.0)

    blank = jnp.zeros((CX, 128), F32)

    def curl_ahead(F, z, k):
        fx, fy, fz = F[0, z], F[1, z], F[2, z]
        rim_y = XR[k, pl.ds(z, 1), :]
        rim_z = XR[k, pl.ds(NZ + z, 1), :]
        lat = YR[k]
        lat_x = pltpu.roll(lat, 127 - z, 1)
        lat_z = pltpu.roll(lat, 127 - NZ - z, 1)

        def up_x(v, rim):
            return jnp.where(last_row, rim, pltpu.roll(v, CX - 1, 0))

        def up_y(v, lateral):
            r = pltpu.roll(v, CY - 1, 1)
            return jnp.concatenate([r[:, 0:128], jnp.where(last_lane, lateral, r[:, 128:256])], axis=1)

        cx = (up_y(fz, lat_z) - fz) - (F[1, z + 1] - fy)
        cy = (F[0, z + 1] - fx) - (up_x(fz, rim_z) - fz)
        cz = (up_x(fy, rim_y) - fy) - (up_y(fx, lat_x) - fx)
        return cx, cy, cz

    def curl_behind(F, z, k):
        fx, fy, fz = F[0, z + 1], F[1, z + 1], F[2, z + 1]
        rim_y = XR[k, pl.ds(z, 1), :]
        rim_z = XR[k, pl.ds(NZ + z, 1), :]
        lat = YR[k]
        lat_x = pltpu.roll(lat, lax.rem(128 - z, 128), 1)
        lat_z = pltpu.roll(lat, 128 - NZ - z, 1)

        def dn_x(v, rim):
            return jnp.where(first_row, rim, pltpu.roll(v, 1, 0))

        def dn_y(v, lateral):
            r = pltpu.roll(v, 1, 1)
            return jnp.concatenate([jnp.where(first_lane, lateral, r[:, 0:128]), r[:, 128:256]], axis=1)

        cx = (fz - dn_y(fz, lat_z)) - (fy - F[1, z])
        cy = (fx - F[0, z]) - (fz - dn_x(fz, rim_z))
        cz = (fy - dn_x(fy, rim_y)) - (fx - dn_y(fx, lat_x))
        return cx, cy, cz

    load_e.wait()

    def pack_e0(z, acc):
        return pack_low(acc, z, 0, E[0, z], E[1, z], E[2, z])

    YS[0] = lax.fori_loop(0, NZ, pack_e0, blank, unroll=NZ)

    pl.semaphore_wait(barrier, n_gx + 1)
    start_rims(0, True)

    def row_copy(send, recv, d, which):
        peer = lax.rem(gx + d, n_gx)
        return pltpu.make_async_remote_copy(
            src_ref=send.at[pl.ds(peer * CAP, CAP)], dst_ref=recv.at[pl.ds(gx * CAP, CAP)],
            send_sem=row_send.at[which, d], recv_sem=row_recv.at[which, d],
            device_id=(peer, gy), device_id_type=MESH)

    for d in range(1, n_gx):
        row_copy(SEND1, RECV1, d, 0).start()
    for s in range(CAP):
        RECV1[gx * CAP + s] = SEND1[gx * CAP + s]

    load_h.wait()
    finish_rims(0, True)

    def h_first(z, acc):
        cx, cy, cz = curl_ahead(E, z, 0)
        hx = H[0, z + 1] - STEP_DT * cx
        hy = H[1, z + 1] - STEP_DT * cy
        hz = H[2, z + 1] - STEP_DT * cz
        H[0, z + 1] = hx
        H[1, z + 1] = hy
        H[2, z + 1] = hz
        return pack_high(acc, z, 1, hx, hy, hz)

    YS[1] = lax.fori_loop(0, NZ, h_first, blank, unroll=NZ)
    start_rims(1, False)

    local_x = cells[1:2, :] - gx * CX
    inside = (local_x >= 0) & (local_x < CX)
    where_zx = jnp.where(inside, cells[0:1, :] * CX + local_x, -1)
    where_y = cells[2:3, :] - gy * CY
    sub_src = lax.broadcasted_iota(jnp.int32, (CX, NSRC), 0)

    def build_hits(z, carry):
        hit = sub_src == where_zx - z * CX
        L[pl.ds(pl.multiple_of(z * CX, CX), CX), :] = jnp.where(hit, 1.0, 0.0).astype(jnp.bfloat16)
        return carry

    lax.fori_loop(0, NZ, build_hits, 0, unroll=NZ)
    hit_y = lax.broadcasted_iota(jnp.int32, (CY, NSRC), 0) == where_y

    for n in range(STEPS):
        for c in range(3):
            row = amp[c, n:n + 1, :]
            high = row.astype(jnp.bfloat16).astype(F32)
            rest = row - high
            mid = rest.astype(jnp.bfloat16).astype(F32)
            low = rest - mid
            total = None
            for part in (high, mid, low):
                cols = jnp.where(hit_y, part, 0.0).astype(jnp.bfloat16)
                term = lax.dot_general(L[...], cols, (((1,), (1,)), ((), ())),
                                       preferred_element_type=F32)
                total = term if total is None else total + term
            S[n * 3 + c] = total.reshape(NZ, CX, CY)

    finish_rims(1, False)

    def c_first(z, carry):
        cx, cy, cz = curl_behind(H, z, 1)
        C1[0, z] = cx
        C1[1, z] = cy
        C1[2, z] = cz
        return carry

    lax.fori_loop(0, NZ, c_first, 0, unroll=NZ)

    for d in range(1, n_gx):
        row_copy(SEND1, RECV1, d, 0).wait()

    def e_first(z, acc):
        inv = 1.0 / (EPS_LOW + EPS_SPAN * RECV1[idx[2 * n_slots + z]])
        INV[z] = inv
        new = []
        for c in range(3):
            value = E[c, z] + STEP_DT * inv * C1[c, z] + STEP_DT * S[c, z]
            E[c, z] = value
            new.append(value)
        return pack_low(acc, z, 2, *new)

    YS[2] = lax.fori_loop(0, NZ, e_first, blank, unroll=NZ)
    start_rims(2, True)
    finish_rims(2, True)

    def h_second(z, acc):
        curls = curl_ahead(E, z, 2)
        new = []
        for c in range(3):
            value = H[c, z + 1] - STEP_DT * curls[c]
            H[c, z + 1] = value
            new.append(value)
        return pack_high(acc, z, 3, *new)

    YS[3] = lax.fori_loop(0, NZ, h_second, blank, unroll=NZ)
    start_rims(3, False)
    save_h = pltpu.make_async_copy(H.at[:, 1:NZ + 1], h_out, local_sem.at[4])
    save_h.start()
    load_t.wait()
    finish_rims(3, False)

    def e_second(z, acc):
        curls = curl_behind(H, z, 3)
        inv = INV[z]
        half_inv = STEP_DT * inv
        grad = None
        new = []
        for c in range(3):
            value = E[c, z] + half_inv * curls[c] + STEP_DT * S[3 + c, z]
            E[c, z] = value
            misfit = value - T[c, z]
            T[c, z] = misfit
            grad = curls[c] * misfit if grad is None else grad + curls[c] * misfit
            value = half_inv * misfit
            G[c, z] = value
            new.append(value)
        EG[z] = grad
        return pack_low(acc, z, 4, *new)

    YS[4] = lax.fori_loop(0, NZ, e_second, blank, unroll=NZ)
    start_rims(4, True)
    save_e = pltpu.make_async_copy(E.at[:, 0:NZ], e_out, local_sem.at[5])
    save_e.start()
    finish_rims(4, True)

    for c in range(3):
        C2[c, 0] = zero_plane

    def adjoint_h(z, acc):
        curls = curl_ahead(G, z, 4)
        for c in range(3):
            C2[c, z + 1] = curls[c]
        return pack_high(acc, z, 5, *curls)

    YS[5] = lax.fori_loop(0, NZ, adjoint_h, blank, unroll=NZ)
    start_rims(5, False)
    finish_rims(5, False)

    def adjoint_e(z, carry):
        curls = curl_behind(C2, z, 5)
        grad = EG[z]
        for c in range(3):
            grad = grad + C1[c, z] * (T[c, z] - STEP_DT * curls[c])
        inv = INV[z]
        EG[z] = (-EPS_SPAN * STEP_DT) * (inv * inv) * grad
        return carry

    lax.fori_loop(0, NZ, adjoint_e, 0, unroll=NZ)

    def pack_planes(slot, carry):
        SEND2[slot] = EG[idx[n_slots + slot]]
        return carry

    lax.fori_loop(0, n_slots, pack_planes, 0, unroll=8)
    for d in range(1, n_gx):
        row_copy(SEND2, RECV2, d, 1).start()
    for s in range(CAP):
        RECV2[gx * CAP + s] = SEND2[gx * CAP + s]
    for d in range(1, n_gx):
        row_copy(SEND2, RECV2, d, 1).wait()

    def unpack(r, carry):
        plane = RECV2[idx[2 * n_slots + NZ + r]]
        ROW[r] = plane[:, 0:128]
        ROW[NZ + r] = plane[:, 128:256]
        return carry

    lax.fori_loop(0, NZ, unpack, 0, unroll=NZ)

    def scale(a, carry):
        own = SL[:, pl.ds(pl.multiple_of(a * CY, CY), CY)]
        parts = [row_lines[pl.ds(half * NZ * CX + a, NZ, stride=CX), :] for half in range(2)]
        D[:, pl.ds(pl.multiple_of((a + 1) * CY, CY), CY)] = jnp.concatenate(parts, axis=1) * own
        return carry

    lax.fori_loop(0, CX, scale, 0, unroll=CX)

    def rows_out(a, carry):
        SL[:, pl.ds(pl.multiple_of(a * CY, CY), CY)] = smooth(D, a)
        return carry

    lax.fori_loop(0, CX, rows_out, 0, unroll=CX)
    save_g = pltpu.make_async_copy(SL, g_out, local_sem.at[6])
    save_g.start()
    save_h.wait()
    save_e.wait()
    save_g.wait()


def solution(mesh):
    n_gx, n_gy = mesh.shape["gx"], mesh.shape["gy"]
    n_slots = n_gx * CAP
    placed = (
        P(None, None, "gx", "gy"),
        P(None, None, "gx", "gy"),
        P(None, None, "gx", "gy"),
        P("gx", "gy"),
        P(None, "gy"),
        P(),
        P(),
    )
    field = (3, NZ, CX, CY)
    padded = (3, NZ + 1, CX, CY)

    def body(e_field, h_field, target, density, region_list, source_cells, source_amp):
        idx = index_tables(region_list, n_gx)
        any_spec = pl.BlockSpec(memory_space=pl.ANY)
        vmem = pl.BlockSpec(memory_space=pltpu.VMEM)
        smem = pl.BlockSpec(memory_space=pltpu.SMEM)

        def run(*refs):
            kernel(n_gx, n_gy, *refs)

        dma = pltpu.SemaphoreType.DMA
        return pl.pallas_call(
            run,
            name="yee_adjoint",
            out_shape=(
                jax.ShapeDtypeStruct(field, F32),
                jax.ShapeDtypeStruct(field, F32),
                jax.ShapeDtypeStruct((NZ, WIDTH), F32),
            ),
            in_specs=[smem, vmem, vmem, any_spec, any_spec, any_spec, any_spec],
            out_specs=(any_spec, any_spec, any_spec),
            scratch_shapes=[
                pltpu.VMEM(padded, F32),
                pltpu.VMEM(padded, F32),
                pltpu.VMEM(field, F32),
                pltpu.VMEM((NZ, WIDTH + 2 * CY), F32),
                pltpu.VMEM((NZ, WIDTH), F32),
                pltpu.VMEM(field, F32),
                pltpu.VMEM(padded, F32),
                pltpu.VMEM(padded, F32),
                pltpu.VMEM((STEPS * 3, NZ, CX, CY), F32),
                pltpu.VMEM((NZ * CX, NSRC), jnp.bfloat16),
                pltpu.VMEM((2 * NZ, CX, 128), F32),
                pltpu.VMEM((NZ, CX, CY), F32),
                pltpu.VMEM((NZ, CX, CY), F32),
                pltpu.VMEM((n_slots, CX, CY), F32),
                pltpu.VMEM((n_slots, CX, CY), F32),
                pltpu.VMEM((n_slots, CX, CY), F32),
                pltpu.VMEM((n_slots, CX, CY), F32),
                pltpu.VMEM((6, 2 * NZ, CY), F32),
                pltpu.VMEM((6, 2 * NZ, CY), F32),
                pltpu.VMEM((6, CX, 128), F32),
                pltpu.VMEM((6, CX, 128), F32),
                dma((7,)),
                dma((2, n_gx)),
                dma((2, n_gx)),
                dma((6,)),
                dma((6,)),
                dma((6,)),
                dma((6,)),
            ],
            compiler_params=pltpu.CompilerParams(collective_id=0, has_side_effects=True),
        )(idx, source_cells, jnp.swapaxes(source_amp, 0, 1), e_field, h_field, target, density)

    return jax.shard_map(
        body,
        mesh=mesh,
        in_specs=placed,
        out_specs=(P(None, None, "gx", "gy"), P(None, None, "gx", "gy"), P("gx", "gy")),
        check_vma=False,
    )
```

```python
import jax
import jax.numpy as jnp
from jax import lax
from jax.experimental import pallas as pl
from jax.experimental.pallas import tpu as pltpu
from jax.sharding import PartitionSpec as P

CX = 16
CY = 256
NZ = 24
STEPS = 2
CAP = 3
NSRC = 512
WIDTH = CX * CY

STEP_DT = 0.5
SHARPNESS = 4.0
MIDPOINT = 0.5
EPS_LOW = 1.0
EPS_SPAN = 3.0
TANH_MID = 0.9640275800758169

F32 = jnp.float32
MESH = pl.DeviceIdType.MESH


def index_tables(region_list, n_gx):
    me = lax.axis_index("gx")
    ids = region_list[:, 0].reshape(n_gx, NZ)
    tile, plane = ids // NZ, ids % NZ
    place = jnp.arange(NZ, dtype=jnp.int32)
    earlier = place[None, :] < place[:, None]
    rank = jnp.sum(
        ((tile[:, :, None] == tile[:, None, :]) & earlier[None]).astype(jnp.int32), axis=2
    )
    own_tile = lax.dynamic_slice_in_dim(tile, me, 1)[0]
    own_rank = lax.dynamic_slice_in_dim(rank, me, 1)[0]
    own_slot = own_tile * CAP + own_rank
    slots = jnp.arange(n_gx * CAP, dtype=jnp.int32)
    send_rows = jnp.sum(jnp.where(own_slot[None, :] == slots[:, None], place[None, :], 0), axis=1)
    shard_slot = jnp.arange(n_gx, dtype=jnp.int32)[:, None] * CAP + rank
    shard_slot_here = jnp.where(tile == me, shard_slot, -1)
    send_planes = jnp.sum(
        jnp.where(shard_slot_here[None] == slots[:, None, None], plane[None], 0), axis=(1, 2)
    )
    take_planes = jnp.sum(
        jnp.where(ids[None] == (me * NZ + place)[:, None, None], shard_slot[None], 0), axis=(1, 2)
    )
    return jnp.concatenate([send_rows, send_planes, take_planes, own_slot]).astype(jnp.int32)


def kernel(n_gx, n_gy, idx, cells, amp, e_hbm, h_hbm, t_hbm, d_hbm, e_out, h_out, g_out,
           E, H, T, D, SL, C1, G, S, L, ROW, INV, EG, SEND1, RECV1, SEND2, RECV2,
           XL, XLR, XH, XHR, YL, YLR, YH, YHR, XC, YC, HSX,
           local_sem, row_send, row_recv, rim_send, rim_recv):
    gx = lax.axis_index("gx")
    gy = lax.axis_index("gy")
    n_slots = n_gx * CAP
    row_lines = ROW.reshape(2 * NZ * CX, 128)

    def turned(x_by, y_by):
        return (lax.rem(gx + x_by + n_gx, n_gx), lax.rem(gy + y_by + n_gy, n_gy))

    others = [(d, 0) for d in range(1, n_gx)] + [(0, 1), (0, -1), (1, -1), (-1, 1)]
    barrier = pltpu.get_barrier_semaphore()
    for x_by, y_by in others:
        pl.semaphore_signal(barrier, inc=1, device_id=turned(x_by, y_by), device_id_type=MESH)

    load_e = pltpu.make_async_copy(e_hbm, E.at[:, 0:NZ], local_sem.at[1])
    load_h = pltpu.make_async_copy(h_hbm, H, local_sem.at[2])
    load_d = pltpu.make_async_copy(d_hbm, D.at[:, CY:CY + WIDTH], local_sem.at[0])
    load_t = pltpu.make_async_copy(t_hbm, T, local_sem.at[3])
    load_e.start()
    load_h.start()
    load_d.start()
    load_t.start()

    zero_plane = jnp.zeros((CX, CY), F32)
    for c in range(3):
        E[c, NZ] = zero_plane
        G[c, NZ] = zero_plane
    D[:, 0:CY] = jnp.zeros((NZ, CY), F32)
    D[:, CY + WIDTH:] = jnp.zeros((NZ, CY), F32)

    lane_wide = lax.broadcasted_iota(jnp.int32, (NZ, CY), 1)
    sub_wide = lax.broadcasted_iota(jnp.int32, (NZ, CY), 0)
    sub = lax.broadcasted_iota(jnp.int32, (CX, CY), 0)
    sub128 = lax.broadcasted_iota(jnp.int32, (CX, 128), 0)
    lane128 = lax.broadcasted_iota(jnp.int32, (CX, 128), 1)
    lane24 = lax.broadcasted_iota(jnp.int32, (NZ, 128), 1)
    first_row, last_row = sub == 0, sub == CX - 1
    first_lane, last_lane = lane128 == 0, lane128 == 127
    wide_first, wide_last = lane_wide == 0, lane_wide == CY - 1
    blank = jnp.zeros((CX, 128), F32)

    def pack_rims(k, z, acc, field, more=None):
        low, high = acc
        fx, fy, fz = field
        XL[k, z:z + 1, :] = fy[0:1, :]
        XL[k, NZ + z:NZ + z + 1, :] = fz[0:1, :]
        for n, v in enumerate((fx, fz)):
            lane = n * NZ + z
            low = jnp.where(lane128 == lane, pltpu.roll(v[:, 0:128], lane, 1), low)
        flat = [fx, fy, fz]
        tall = [fx, fy, fz]
        if more is not None:
            flat += [more[1], more[2]]
            tall += [more[0], more[2]]
        for n, v in enumerate(flat):
            XH[k, n * NZ + z:n * NZ + z + 1, :] = v[CX - 1:CX, :]
        for n, v in enumerate(tall):
            lane = n * NZ + z
            high = jnp.where(lane128 == lane, pltpu.roll(v[:, 128:256], lane + 1, 1), high)
        return low, high

    def rim_copies(k):
        tall = (5 if k == 0 else 3) * NZ
        moves = [
            (XH.at[k, 0:tall], XHR.at[k, 0:tall], (1, 0)),
            (XL.at[k], XLR.at[k], (-1, 0)),
            (XH.at[k, 0:NZ, 0:128], XC.at[k], (1, -1)),
            (YH.at[k, 0:8], YC.at[k], (-1, 1)),
            (YH.at[k], YHR.at[k], (0, 1)),
            (YL.at[k], YLR.at[k], (0, -1)),
        ]
        return [
            pltpu.make_async_remote_copy(
                src_ref=src, dst_ref=dst, send_sem=rim_send.at[k, n], recv_sem=rim_recv.at[k, n],
                device_id=turned(*by), device_id_type=MESH)
            for n, (src, dst, by) in enumerate(moves)
        ]

    def start_rims(k, acc):
        YL[k], YH[k] = acc
        for copy in rim_copies(k):
            copy.start()

    def keep(inside):
        return jnp.where(inside, 1.0, 0.0)

    has_low_x, has_high_x = keep(gx > 0), keep(gx < n_gx - 1)
    has_low_y, has_high_y = keep(gy > 0), keep(gy < n_gy - 1)

    def finish_rims(k):
        for copy in rim_copies(k):
            copy.wait()
        XLR[k] = XLR[k] * has_high_x

    def strips(k):
        ex, ey, ez = (XHR[k, n * NZ:n * NZ + NZ, :] for n in range(3))
        ey_own, ez_own = XL[k, 0:NZ, :], XL[k, NZ:2 * NZ, :]
        corner = pltpu.roll(XC[k], 127, 1) * has_high_y
        turned_y = pltpu.roll(ex, CY - 1, 1)
        upper = jnp.where(lane24 == 127, corner, turned_y[:, 128:256])
        ahead_y = jnp.concatenate([turned_y[:, 0:128], upper], axis=1) - ex
        ahead_z = jnp.where(sub_wide == NZ - 1, 0.0, pltpu.roll(ex, NZ - 1, 0)) - ex
        flat_y = ahead_z - (ez_own - ez)
        flat_z = (ey_own - ey) - ahead_y

        tall, own = YHR[k], YL[k]
        next_z = jnp.where(lane128 == NZ - 1, 0.0, pltpu.roll(tall, 128 - NZ - 1, 1))
        tall_x = (pltpu.roll(own, 128 - NZ, 1) - pltpu.roll(tall, 128 - 2 * NZ, 1)) - (
            next_z - pltpu.roll(tall, 128 - NZ, 1))
        next_x = jnp.where(sub128 == CX - 1, YC[k, 0:1, :] * has_high_x, pltpu.roll(tall, CX - 1, 0))
        tall_z = (next_x - tall) - (pltpu.roll(own, NZ, 1) - pltpu.roll(tall, NZ, 1))
        return flat_y, flat_z, jnp.where(lane128 < NZ, tall_x, tall_z)

    def curl_ahead(here, above, k, z, lat):
        fx, fy, fz = here
        rim_y = XLR[k, z:z + 1, :]
        rim_z = XLR[k, NZ + z:NZ + z + 1, :]
        lat_x = pltpu.roll(lat, 127 - z, 1)
        lat_z = pltpu.roll(lat, 127 - NZ - z, 1)

        def up_x(v, rim):
            return jnp.where(last_row, rim, pltpu.roll(v, CX - 1, 0))

        def up_y(v, lateral):
            r = pltpu.roll(v, CY - 1, 1)
            return jnp.concatenate([r[:, 0:128], jnp.where(last_lane, lateral, r[:, 128:256])], axis=1)

        return (
            (up_y(fz, lat_z) - fz) - (above[1] - fy),
            (above[0] - fx) - (up_x(fz, rim_z) - fz),
            (up_x(fy, rim_y) - fy) - (up_y(fx, lat_x) - fx),
        )

    def curl_behind(here, below, z, lat):
        fx, fy, fz = here
        rim_y = HSX[z:z + 1, :]
        rim_z = HSX[NZ + z:NZ + z + 1, :]
        lat_x = pltpu.roll(lat, (128 - z) % 128, 1)
        lat_z = pltpu.roll(lat, 128 - NZ - z, 1)

        def dn_x(v, rim):
            return jnp.where(first_row, rim, pltpu.roll(v, 1, 0))

        def dn_y(v, lateral):
            r = pltpu.roll(v, 1, 1)
            return jnp.concatenate([jnp.where(first_lane, lateral, r[:, 0:128]), r[:, 128:256]], axis=1)

        return (
            (fz - dn_y(fz, lat_z)) - (fy - below[1]),
            (fx - below[0]) - (fz - dn_x(fz, rim_z)),
            (fy - dn_x(fy, rim_y)) - (fx - dn_y(fx, lat_x)),
        )

    def plane(ref, z):
        return tuple(ref[c, z] for c in range(3))

    load_e.wait()
    load_h.wait()
    acc = (blank, blank)
    for z in range(NZ):
        acc = pack_rims(0, z, acc, plane(E, z), plane(H, z))
    pl.semaphore_wait(barrier, len(others))
    start_rims(0, acc)

    def smooth(ref, a):
        at = (a + 1) * CY
        mid = ref[:, at:at + CY]
        low = ref[:, at - CY:at]
        high = ref[:, at + CY:at + 2 * CY]
        right = jnp.where(wide_last, 0.0, pltpu.roll(mid, CY - 1, 1))
        left = jnp.where(wide_first, 0.0, pltpu.roll(mid, 1, 1))
        return 0.5 * mid + 0.125 * (high + low + right + left)

    load_d.wait()
    for a in range(CX):
        inner = jnp.tanh(SHARPNESS * (smooth(D, a) - MIDPOINT))
        SL[:, a * CY:a * CY + CY] = SHARPNESS * (1.0 - inner * inner) / (2.0 * TANH_MID)
        projected = (TANH_MID + inner) / (2.0 * TANH_MID)
        for half in range(2):
            row_lines[pl.ds(half * NZ * CX + a, NZ, stride=CX), :] = projected[:, half * 128:half * 128 + 128]

    def pack_rows(slot, carry):
        row = idx[slot]
        SEND1[slot, :, 0:128] = ROW[row]
        SEND1[slot, :, 128:256] = ROW[NZ + row]
        return carry

    lax.fori_loop(0, n_slots, pack_rows, 0, unroll=8)

    def row_copy(send, recv, d, which):
        peer = lax.rem(gx + d, n_gx)
        return pltpu.make_async_remote_copy(
            src_ref=send.at[pl.ds(peer * CAP, CAP)], dst_ref=recv.at[pl.ds(gx * CAP, CAP)],
            send_sem=row_send.at[which, d], recv_sem=row_recv.at[which, d],
            device_id=(peer, gy), device_id_type=MESH)

    for d in range(1, n_gx):
        row_copy(SEND1, RECV1, d, 0).start()
    for s in range(CAP):
        RECV1[gx * CAP + s] = SEND1[gx * CAP + s]

    local_x = cells[1:2, :] - gx * CX
    inside = (local_x >= 0) & (local_x < CX)
    where_zx = jnp.where(inside, cells[0:1, :] * CX + local_x, -1)
    where_y = cells[2:3, :] - gy * CY
    sub_src = lax.broadcasted_iota(jnp.int32, (CX, NSRC), 0)
    for z in range(NZ):
        hit = sub_src == where_zx - z * CX
        L[z * CX:z * CX + CX, :] = jnp.where(hit, 1.0, 0.0).astype(jnp.bfloat16)
    hit_y = lax.broadcasted_iota(jnp.int32, (CY, NSRC), 0) == where_y

    for n in range(STEPS):
        for c in range(3):
            row = amp[c, n:n + 1, :]
            high = row.astype(jnp.bfloat16).astype(F32)
            rest = row - high
            mid = rest.astype(jnp.bfloat16).astype(F32)
            low = rest - mid
            total = None
            for part in (high, mid, low):
                cols = jnp.where(hit_y, part, 0.0).astype(jnp.bfloat16)
                term = lax.dot_general(L[...], cols, (((1,), (1,)), ((), ())),
                                       preferred_element_type=F32)
                total = term if total is None else total + term
            S[n * 3 + c] = total.reshape(NZ, CX, CY)

    finish_rims(0)
    flat_y, flat_z, tall = strips(0)
    HSX[0:NZ, :] = (XHR[0, 3 * NZ:4 * NZ, :] - STEP_DT * flat_y) * has_low_x
    HSX[NZ:2 * NZ, :] = (XHR[0, 4 * NZ:5 * NZ, :] - STEP_DT * flat_z) * has_low_x
    lat_h = (pltpu.roll(YHR[0], 128 - 3 * NZ, 1) - STEP_DT * tall) * has_low_y
    lat_e = YLR[0] * has_high_y
    below = (zero_plane, zero_plane, None)
    for z in range(NZ):
        curls = curl_ahead(plane(E, z), plane(E, z + 1), 0, z, lat_e)
        here = tuple(H[c, z] - STEP_DT * curls[c] for c in range(3))
        for c in range(3):
            H[c, z] = here[c]
        curls = curl_behind(here, below, z, lat_h)
        for c in range(3):
            C1[c, z] = curls[c]
        below = here

    for d in range(1, n_gx):
        row_copy(SEND1, RECV1, d, 0).wait()

    acc = (blank, blank)
    for z in range(NZ):
        inv = 1.0 / (EPS_LOW + EPS_SPAN * RECV1[idx[2 * n_slots + z]])
        INV[z] = inv
        here = tuple(E[c, z] + STEP_DT * inv * C1[c, z] + STEP_DT * S[c, z] for c in range(3))
        for c in range(3):
            E[c, z] = here[c]
        acc = pack_rims(1, z, acc, here)
    start_rims(1, acc)
    load_t.wait()
    finish_rims(1)
    flat_y, flat_z, tall = strips(1)
    HSX[0:NZ, :] = (HSX[0:NZ, :] - STEP_DT * flat_y) * has_low_x
    HSX[NZ:2 * NZ, :] = (HSX[NZ:2 * NZ, :] - STEP_DT * flat_z) * has_low_x
    lat_h = (lat_h - STEP_DT * tall) * has_low_y
    lat_e = YLR[1] * has_high_y

    acc = (blank, blank)
    below = (zero_plane, zero_plane, None)
    for z in range(NZ):
        curls = curl_ahead(plane(E, z), plane(E, z + 1), 1, z, lat_e)
        here = tuple(H[c, z] - STEP_DT * curls[c] for c in range(3))
        for c in range(3):
            H[c, z] = here[c]
        curls = curl_behind(here, below, z, lat_h)
        below = here
        half_inv = STEP_DT * INV[z]
        grad = None
        scaled = []
        for c in range(3):
            value = E[c, z] + half_inv * curls[c] + STEP_DT * S[3 + c, z]
            E[c, z] = value
            misfit = value - T[c, z]
            T[c, z] = misfit
            grad = curls[c] * misfit if grad is None else grad + curls[c] * misfit
            value = half_inv * misfit
            G[c, z] = value
            scaled.append(value)
        EG[z] = grad
        acc = pack_rims(2, z, acc, scaled)
    start_rims(2, acc)
    save_h = pltpu.make_async_copy(H, h_out, local_sem.at[4])
    save_h.start()
    save_e = pltpu.make_async_copy(E.at[:, 0:NZ], e_out, local_sem.at[5])
    save_e.start()
    finish_rims(2)
    flat_y, flat_z, tall = strips(2)
    HSX[0:NZ, :] = flat_y * has_low_x
    HSX[NZ:2 * NZ, :] = flat_z * has_low_x
    lat_h = tall * has_low_y
    lat_e = YLR[2] * has_high_y

    below = (zero_plane, zero_plane, None)
    for z in range(NZ):
        here = curl_ahead(plane(G, z), plane(G, z + 1), 2, z, lat_e)
        curls = curl_behind(here, below, z, lat_h)
        below = here
        grad = EG[z]
        for c in range(3):
            grad = grad + C1[c, z] * (T[c, z] - STEP_DT * curls[c])
        inv = INV[z]
        EG[z] = (-EPS_SPAN * STEP_DT) * (inv * inv) * grad

    def pack_planes(slot, carry):
        SEND2[slot] = EG[idx[n_slots + slot]]
        return carry

    lax.fori_loop(0, n_slots, pack_planes, 0, unroll=8)
    for d in range(1, n_gx):
        row_copy(SEND2, RECV2, d, 1).start()
    for s in range(CAP):
        RECV2[gx * CAP + s] = SEND2[gx * CAP + s]
    for d in range(1, n_gx):
        row_copy(SEND2, RECV2, d, 1).wait()

    for r in range(NZ):
        rows = RECV2[idx[2 * n_slots + NZ + r]]
        ROW[r] = rows[:, 0:128]
        ROW[NZ + r] = rows[:, 128:256]
    for a in range(CX):
        parts = [row_lines[pl.ds(half * NZ * CX + a, NZ, stride=CX), :] for half in range(2)]
        D[:, (a + 1) * CY:(a + 2) * CY] = jnp.concatenate(parts, axis=1) * SL[:, a * CY:a * CY + CY]
    for a in range(CX):
        SL[:, a * CY:a * CY + CY] = smooth(D, a)
    save_g = pltpu.make_async_copy(SL, g_out, local_sem.at[6])
    save_g.start()
    save_h.wait()
    save_e.wait()
    save_g.wait()


def solution(mesh):
    n_gx, n_gy = mesh.shape["gx"], mesh.shape["gy"]
    n_slots = n_gx * CAP
    placed = (
        P(None, None, "gx", "gy"),
        P(None, None, "gx", "gy"),
        P(None, None, "gx", "gy"),
        P("gx", "gy"),
        P(None, "gy"),
        P(),
        P(),
    )
    field = (3, NZ, CX, CY)
    padded = (3, NZ + 1, CX, CY)

    def body(e_field, h_field, target, density, region_list, source_cells, source_amp):
        idx = index_tables(region_list, n_gx)
        any_spec = pl.BlockSpec(memory_space=pl.ANY)
        vmem = pl.BlockSpec(memory_space=pltpu.VMEM)
        smem = pl.BlockSpec(memory_space=pltpu.SMEM)

        def run(*refs):
            kernel(n_gx, n_gy, *refs)

        dma = pltpu.SemaphoreType.DMA
        return pl.pallas_call(
            run,
            name="yee_adjoint",
            out_shape=(
                jax.ShapeDtypeStruct(field, F32),
                jax.ShapeDtypeStruct(field, F32),
                jax.ShapeDtypeStruct((NZ, WIDTH), F32),
            ),
            in_specs=[smem, vmem, vmem, any_spec, any_spec, any_spec, any_spec],
            out_specs=(any_spec, any_spec, any_spec),
            scratch_shapes=[
                pltpu.VMEM(padded, F32),
                pltpu.VMEM(field, F32),
                pltpu.VMEM(field, F32),
                pltpu.VMEM((NZ, WIDTH + 2 * CY), F32),
                pltpu.VMEM((NZ, WIDTH), F32),
                pltpu.VMEM(field, F32),
                pltpu.VMEM(padded, F32),
                pltpu.VMEM((STEPS * 3, NZ, CX, CY), F32),
                pltpu.VMEM((NZ * CX, NSRC), jnp.bfloat16),
                pltpu.VMEM((2 * NZ, CX, 128), F32),
                pltpu.VMEM((NZ, CX, CY), F32),
                pltpu.VMEM((NZ, CX, CY), F32),
                pltpu.VMEM((n_slots, CX, CY), F32),
                pltpu.VMEM((n_slots, CX, CY), F32),
                pltpu.VMEM((n_slots, CX, CY), F32),
                pltpu.VMEM((n_slots, CX, CY), F32),
                pltpu.VMEM((3, 2 * NZ, CY), F32),
                pltpu.VMEM((3, 2 * NZ, CY), F32),
                pltpu.VMEM((3, 5 * NZ, CY), F32),
                pltpu.VMEM((3, 5 * NZ, CY), F32),
                pltpu.VMEM((3, CX, 128), F32),
                pltpu.VMEM((3, CX, 128), F32),
                pltpu.VMEM((3, CX, 128), F32),
                pltpu.VMEM((3, CX, 128), F32),
                pltpu.VMEM((3, NZ, 128), F32),
                pltpu.VMEM((3, 8, 128), F32),
                pltpu.VMEM((2 * NZ, CY), F32),
                dma((7,)),
                dma((2, n_gx)),
                dma((2, n_gx)),
                dma((3, 6)),
                dma((3, 6)),
            ],
            compiler_params=pltpu.CompilerParams(collective_id=0, has_side_effects=True),
        )(idx, source_cells, jnp.swapaxes(source_amp, 0, 1), e_field, h_field, target, density)

    return jax.shard_map(
        body,
        mesh=mesh,
        in_specs=placed,
        out_specs=(P(None, None, "gx", "gy"), P(None, None, "gx", "gy"), P("gx", "gy")),
        check_vma=False,
    )
```

```python
import jax
import jax.numpy as jnp
from jax import lax
from jax.experimental import pallas as pl
from jax.experimental.pallas import tpu as pltpu
from jax.sharding import PartitionSpec as P

CX = 16
CY = 256
NZ = 24
STEPS = 2
CAP = 3
NSRC = 512
WIDTH = CX * CY

STEP_DT = 0.5
SHARPNESS = 4.0
MIDPOINT = 0.5
EPS_LOW = 1.0
EPS_SPAN = 3.0
TANH_MID = 0.9640275800758169

F32 = jnp.float32
MESH = pl.DeviceIdType.MESH


def kernel(n_gx, n_gy, listed, cells, amp, e_hbm, h_hbm, t_hbm, d_hbm, e_out, h_out, g_out,
           E, H, T, D, SL, C1, G, S, L, ROW, INV, EG, SEND1, RECV1, SEND2, RECV2,
           XL, XLR, XH, XHR, YL, YLR, YH, YHR, XC, YC, HSX, TV, idx,
           local_sem, row_send, row_recv, rim_send, rim_recv):
    gx = lax.axis_index("gx")
    gy = lax.axis_index("gy")
    n_slots = n_gx * CAP
    row_lines = ROW.reshape(2 * NZ * CX, 128)

    def turned(x_by, y_by):
        return (lax.rem(gx + x_by + n_gx, n_gx), lax.rem(gy + y_by + n_gy, n_gy))

    others = [(d, 0) for d in range(1, n_gx)] + [(0, 1), (0, -1), (1, -1), (-1, 1)]
    barrier = pltpu.get_barrier_semaphore()
    for x_by, y_by in others:
        pl.semaphore_signal(barrier, inc=1, device_id=turned(x_by, y_by), device_id_type=MESH)

    load_e = pltpu.make_async_copy(e_hbm, E.at[:, 0:NZ], local_sem.at[1])
    load_h = pltpu.make_async_copy(h_hbm, H, local_sem.at[2])
    load_d = pltpu.make_async_copy(d_hbm, D.at[:, CY:CY + WIDTH], local_sem.at[0])
    load_t = pltpu.make_async_copy(t_hbm, T, local_sem.at[3])
    load_d.start()
    load_e.start()
    load_h.start()
    load_t.start()

    n_rows = n_gx * NZ
    ids = jnp.broadcast_to(listed[...], (8, n_rows))
    row_at = lax.broadcasted_iota(jnp.int32, (8, n_rows), 1)
    tile = (ids * 2731) >> 16
    shard = (row_at * 2731) >> 16
    place = row_at - shard * NZ
    rank = jnp.zeros((8, n_rows), jnp.int32)
    for d in range(1, NZ):
        same = (pltpu.roll(tile, d, 1) == tile) & (place >= d)
        rank = rank + jnp.where(same, 1, 0)
    to_slot = tile * CAP + rank
    from_slot = shard * CAP + rank

    def hits(values, count):
        at = lax.broadcasted_iota(jnp.int32, (count, n_rows), 0)
        return jnp.where(jnp.broadcast_to(values[0:1, :], (count, n_rows)) == at, 1.0, 0.0)

    table = jnp.concatenate([
        hits(jnp.where(shard == gx, to_slot, -1), n_slots),
        hits(jnp.where(tile == gx, from_slot, -1), n_slots),
        hits(ids - gx * NZ, NZ),
        hits(row_at - gx * NZ, NZ),
        jnp.zeros((256 - 2 * n_slots - 2 * NZ, n_rows), F32),
    ], axis=0).astype(jnp.bfloat16)
    row8 = lax.broadcasted_iota(jnp.int32, (8, n_rows), 0)
    found = jnp.where(row8 == 0, place, jnp.where(
        row8 == 1, ids - tile * NZ, jnp.where(row8 == 2, from_slot, to_slot)))
    entries = lax.dot_general(
        found.astype(F32).astype(jnp.bfloat16), table, (((1,), (1,)), ((), ())),
        preferred_element_type=F32).astype(jnp.int32)
    row256 = lax.broadcasted_iota(jnp.int32, (8, 256), 0)
    TV[...] = jnp.clip(entries, 0, jnp.where(row256 < 2, NZ - 1, n_slots - 1))
    load_idx = pltpu.make_async_copy(TV, idx, local_sem.at[7])
    load_idx.start()

    zero_plane = jnp.zeros((CX, CY), F32)
    for c in range(3):
        E[c, NZ] = zero_plane
        G[c, NZ] = zero_plane
    D[:, 0:CY] = jnp.zeros((NZ, CY), F32)
    D[:, CY + WIDTH:] = jnp.zeros((NZ, CY), F32)

    lane_wide = lax.broadcasted_iota(jnp.int32, (NZ, CY), 1)
    sub_wide = lax.broadcasted_iota(jnp.int32, (NZ, CY), 0)
    sub = lax.broadcasted_iota(jnp.int32, (CX, CY), 0)
    sub128 = lax.broadcasted_iota(jnp.int32, (CX, 128), 0)
    lane128 = lax.broadcasted_iota(jnp.int32, (CX, 128), 1)
    lane24 = lax.broadcasted_iota(jnp.int32, (NZ, 128), 1)
    first_row, last_row = sub == 0, sub == CX - 1
    first_lane, last_lane = lane128 == 0, lane128 == 127
    wide_first, wide_last = lane_wide == 0, lane_wide == CY - 1
    blank = jnp.zeros((CX, 128), F32)

    def pack_rims(k, z, acc, field, more=None):
        low, high = acc
        fx, fy, fz = field
        XL[k, z:z + 1, :] = fy[0:1, :]
        XL[k, NZ + z:NZ + z + 1, :] = fz[0:1, :]
        for n, v in enumerate((fx, fz)):
            lane = n * NZ + z
            low = jnp.where(lane128 == lane, pltpu.roll(v[:, 0:128], lane, 1), low)
        flat = [fx, fy, fz]
        tall = [fx, fy, fz]
        if more is not None:
            flat += [more[1], more[2]]
            tall += [more[0], more[2]]
        for n, v in enumerate(flat):
            XH[k, n * NZ + z:n * NZ + z + 1, :] = v[CX - 1:CX, :]
        for n, v in enumerate(tall):
            lane = n * NZ + z
            high = jnp.where(lane128 == lane, pltpu.roll(v[:, 128:256], lane + 1, 1), high)
        return low, high

    def rim_copies(k):
        tall = (5 if k == 0 else 3) * NZ
        moves = [
            (XH.at[k, 0:tall], XHR.at[k, 0:tall], (1, 0)),
            (XL.at[k], XLR.at[k], (-1, 0)),
            (XH.at[k, 0:NZ, 0:128], XC.at[k], (1, -1)),
            (YH.at[k, 0:8], YC.at[k], (-1, 1)),
            (YH.at[k], YHR.at[k], (0, 1)),
            (YL.at[k], YLR.at[k], (0, -1)),
        ]
        return [
            pltpu.make_async_remote_copy(
                src_ref=src, dst_ref=dst, send_sem=rim_send.at[k, n], recv_sem=rim_recv.at[k, n],
                device_id=turned(*by), device_id_type=MESH)
            for n, (src, dst, by) in enumerate(moves)
        ]

    def start_rims(k, acc):
        YL[k], YH[k] = acc
        for copy in rim_copies(k):
            copy.start()

    def keep(inside):
        return jnp.where(inside, 1.0, 0.0)

    has_low_x, has_high_x = keep(gx > 0), keep(gx < n_gx - 1)
    has_low_y, has_high_y = keep(gy > 0), keep(gy < n_gy - 1)

    def finish_rims(k):
        for copy in rim_copies(k):
            copy.wait()
        XLR[k] = XLR[k] * has_high_x

    def strips(k):
        ex, ey, ez = (XHR[k, n * NZ:n * NZ + NZ, :] for n in range(3))
        ey_own, ez_own = XL[k, 0:NZ, :], XL[k, NZ:2 * NZ, :]
        corner = pltpu.roll(XC[k], 127, 1) * has_high_y
        turned_y = pltpu.roll(ex, CY - 1, 1)
        upper = jnp.where(lane24 == 127, corner, turned_y[:, 128:256])
        ahead_y = jnp.concatenate([turned_y[:, 0:128], upper], axis=1) - ex
        ahead_z = jnp.where(sub_wide == NZ - 1, 0.0, pltpu.roll(ex, NZ - 1, 0)) - ex
        flat_y = ahead_z - (ez_own - ez)
        flat_z = (ey_own - ey) - ahead_y

        tall, own = YHR[k], YL[k]
        next_z = jnp.where(lane128 == NZ - 1, 0.0, pltpu.roll(tall, 128 - NZ - 1, 1))
        tall_x = (pltpu.roll(own, 128 - NZ, 1) - pltpu.roll(tall, 128 - 2 * NZ, 1)) - (
            next_z - pltpu.roll(tall, 128 - NZ, 1))
        next_x = jnp.where(sub128 == CX - 1, YC[k, 0:1, :] * has_high_x, pltpu.roll(tall, CX - 1, 0))
        tall_z = (next_x - tall) - (pltpu.roll(own, NZ, 1) - pltpu.roll(tall, NZ, 1))
        return flat_y, flat_z, jnp.where(lane128 < NZ, tall_x, tall_z)

    def curl_ahead(here, above, k, z, lat):
        fx, fy, fz = here
        rim_y = XLR[k, z:z + 1, :]
        rim_z = XLR[k, NZ + z:NZ + z + 1, :]
        lat_x = pltpu.roll(lat, 127 - z, 1)
        lat_z = pltpu.roll(lat, 127 - NZ - z, 1)

        def up_x(v, rim):
            return jnp.where(last_row, rim, pltpu.roll(v, CX - 1, 0))

        def up_y(v, lateral):
            r = pltpu.roll(v, CY - 1, 1)
            return jnp.concatenate([r[:, 0:128], jnp.where(last_lane, lateral, r[:, 128:256])], axis=1)

        return (
            (up_y(fz, lat_z) - fz) - (above[1] - fy),
            (above[0] - fx) - (up_x(fz, rim_z) - fz),
            (up_x(fy, rim_y) - fy) - (up_y(fx, lat_x) - fx),
        )

    def curl_behind(here, below, z, lat):
        fx, fy, fz = here
        rim_y = HSX[z:z + 1, :]
        rim_z = HSX[NZ + z:NZ + z + 1, :]
        lat_x = pltpu.roll(lat, (128 - z) % 128, 1)
        lat_z = pltpu.roll(lat, 128 - NZ - z, 1)

        def dn_x(v, rim):
            return jnp.where(first_row, rim, pltpu.roll(v, 1, 0))

        def dn_y(v, lateral):
            r = pltpu.roll(v, 1, 1)
            return jnp.concatenate([jnp.where(first_lane, lateral, r[:, 0:128]), r[:, 128:256]], axis=1)

        return (
            (fz - dn_y(fz, lat_z)) - (fy - below[1]),
            (fx - below[0]) - (fz - dn_x(fz, rim_z)),
            (fy - dn_x(fy, rim_y)) - (fx - dn_y(fx, lat_x)),
        )

    def plane(ref, z):
        return tuple(ref[c, z] for c in range(3))

    def smooth(ref, a):
        at = (a + 1) * CY
        mid = ref[:, at:at + CY]
        low = ref[:, at - CY:at]
        high = ref[:, at + CY:at + 2 * CY]
        right = jnp.where(wide_last, 0.0, pltpu.roll(mid, CY - 1, 1))
        left = jnp.where(wide_first, 0.0, pltpu.roll(mid, 1, 1))
        return 0.5 * mid + 0.125 * (high + low + right + left)

    load_d.wait()
    for a in range(CX):
        inner = jnp.tanh(SHARPNESS * (smooth(D, a) - MIDPOINT))
        SL[:, a * CY:a * CY + CY] = SHARPNESS * (1.0 - inner * inner) / (2.0 * TANH_MID)
        projected = (TANH_MID + inner) / (2.0 * TANH_MID)
        for half in range(2):
            row_lines[pl.ds(half * NZ * CX + a, NZ, stride=CX), :] = projected[:, half * 128:half * 128 + 128]

    def pack_rows(slot, carry):
        row = jnp.clip(idx[0, slot], 0, NZ - 1)
        SEND1[slot, :, 0:128] = ROW[row]
        SEND1[slot, :, 128:256] = ROW[NZ + row]
        return carry

    load_idx.wait()
    lax.fori_loop(0, n_slots, pack_rows, 0, unroll=8)

    load_e.wait()
    load_h.wait()
    acc = (blank, blank)
    for z in range(NZ):
        acc = pack_rims(0, z, acc, plane(E, z), plane(H, z))
    pl.semaphore_wait(barrier, len(others))
    start_rims(0, acc)

    def row_copy(send, recv, d, which):
        peer = lax.rem(gx + d, n_gx)
        return pltpu.make_async_remote_copy(
            src_ref=send.at[pl.ds(peer * CAP, CAP)], dst_ref=recv.at[pl.ds(gx * CAP, CAP)],
            send_sem=row_send.at[which, d], recv_sem=row_recv.at[which, d],
            device_id=(peer, gy), device_id_type=MESH)

    for d in range(1, n_gx):
        row_copy(SEND1, RECV1, d, 0).start()
    for s in range(CAP):
        RECV1[gx * CAP + s] = SEND1[gx * CAP + s]

    local_x = cells[1:2, :] - gx * CX
    inside = (local_x >= 0) & (local_x < CX)
    where_zx = jnp.where(inside, cells[0:1, :] * CX + local_x, -1)
    where_y = cells[2:3, :] - gy * CY
    sub_src = lax.broadcasted_iota(jnp.int32, (CX, NSRC), 0)
    for z in range(NZ):
        hit = sub_src == where_zx - z * CX
        L[z * CX:z * CX + CX, :] = jnp.where(hit, 1.0, 0.0).astype(jnp.bfloat16)
    hit_y = lax.broadcasted_iota(jnp.int32, (CY, NSRC), 0) == where_y

    for n in range(STEPS):
        for c in range(3):
            row = amp[c, n:n + 1, :]
            high = row.astype(jnp.bfloat16).astype(F32)
            rest = row - high
            mid = rest.astype(jnp.bfloat16).astype(F32)
            low = rest - mid
            total = None
            for part in (high, mid, low):
                cols = jnp.where(hit_y, part, 0.0).astype(jnp.bfloat16)
                term = lax.dot_general(L[...], cols, (((1,), (1,)), ((), ())),
                                       preferred_element_type=F32)
                total = term if total is None else total + term
            S[n * 3 + c] = total.reshape(NZ, CX, CY)

    finish_rims(0)
    flat_y, flat_z, tall = strips(0)
    HSX[0:NZ, :] = (XHR[0, 3 * NZ:4 * NZ, :] - STEP_DT * flat_y) * has_low_x
    HSX[NZ:2 * NZ, :] = (XHR[0, 4 * NZ:5 * NZ, :] - STEP_DT * flat_z) * has_low_x
    lat_h = (pltpu.roll(YHR[0], 128 - 3 * NZ, 1) - STEP_DT * tall) * has_low_y
    lat_e = YLR[0] * has_high_y
    below = (zero_plane, zero_plane, None)
    for z in range(NZ):
        curls = curl_ahead(plane(E, z), plane(E, z + 1), 0, z, lat_e)
        here = tuple(H[c, z] - STEP_DT * curls[c] for c in range(3))
        for c in range(3):
            H[c, z] = here[c]
        curls = curl_behind(here, below, z, lat_h)
        for c in range(3):
            C1[c, z] = curls[c]
        below = here

    for d in range(1, n_gx):
        row_copy(SEND1, RECV1, d, 0).wait()

    acc = (blank, blank)
    for z in range(NZ):
        inv = 1.0 / (EPS_LOW + EPS_SPAN * RECV1[jnp.clip(idx[2, 2 * n_slots + z], 0, n_slots - 1)])
        INV[z] = inv
        here = tuple(E[c, z] + STEP_DT * inv * C1[c, z] + STEP_DT * S[c, z] for c in range(3))
        for c in range(3):
            E[c, z] = here[c]
        acc = pack_rims(1, z, acc, here)
    start_rims(1, acc)
    load_t.wait()
    finish_rims(1)
    flat_y, flat_z, tall = strips(1)
    HSX[0:NZ, :] = (HSX[0:NZ, :] - STEP_DT * flat_y) * has_low_x
    HSX[NZ:2 * NZ, :] = (HSX[NZ:2 * NZ, :] - STEP_DT * flat_z) * has_low_x
    lat_h = (lat_h - STEP_DT * tall) * has_low_y
    lat_e = YLR[1] * has_high_y

    acc = (blank, blank)
    below = (zero_plane, zero_plane, None)
    for z in range(NZ):
        curls = curl_ahead(plane(E, z), plane(E, z + 1), 1, z, lat_e)
        here = tuple(H[c, z] - STEP_DT * curls[c] for c in range(3))
        for c in range(3):
            H[c, z] = here[c]
        curls = curl_behind(here, below, z, lat_h)
        below = here
        half_inv = STEP_DT * INV[z]
        grad = None
        scaled = []
        for c in range(3):
            value = E[c, z] + half_inv * curls[c] + STEP_DT * S[3 + c, z]
            E[c, z] = value
            misfit = value - T[c, z]
            T[c, z] = misfit
            grad = curls[c] * misfit if grad is None else grad + curls[c] * misfit
            value = half_inv * misfit
            G[c, z] = value
            scaled.append(value)
        EG[z] = grad
        acc = pack_rims(2, z, acc, scaled)
    start_rims(2, acc)
    save_h = pltpu.make_async_copy(H, h_out, local_sem.at[4])
    save_h.start()
    save_e = pltpu.make_async_copy(E.at[:, 0:NZ], e_out, local_sem.at[5])
    save_e.start()
    finish_rims(2)
    flat_y, flat_z, tall = strips(2)
    HSX[0:NZ, :] = flat_y * has_low_x
    HSX[NZ:2 * NZ, :] = flat_z * has_low_x
    lat_h = tall * has_low_y
    lat_e = YLR[2] * has_high_y

    below = (zero_plane, zero_plane, None)
    for z in range(NZ):
        here = curl_ahead(plane(G, z), plane(G, z + 1), 2, z, lat_e)
        curls = curl_behind(here, below, z, lat_h)
        below = here
        grad = EG[z]
        for c in range(3):
            grad = grad + C1[c, z] * (T[c, z] - STEP_DT * curls[c])
        inv = INV[z]
        EG[z] = (-EPS_SPAN * STEP_DT) * (inv * inv) * grad

    def pack_planes(slot, carry):
        SEND2[slot] = EG[jnp.clip(idx[1, n_slots + slot], 0, NZ - 1)]
        return carry

    lax.fori_loop(0, n_slots, pack_planes, 0, unroll=8)
    for d in range(1, n_gx):
        row_copy(SEND2, RECV2, d, 1).start()
    for s in range(CAP):
        RECV2[gx * CAP + s] = SEND2[gx * CAP + s]
    for d in range(1, n_gx):
        row_copy(SEND2, RECV2, d, 1).wait()

    for r in range(NZ):
        rows = RECV2[jnp.clip(idx[3, 2 * n_slots + NZ + r], 0, n_slots - 1)]
        ROW[r] = rows[:, 0:128]
        ROW[NZ + r] = rows[:, 128:256]
    for a in range(CX):
        parts = [row_lines[pl.ds(half * NZ * CX + a, NZ, stride=CX), :] for half in range(2)]
        D[:, (a + 1) * CY:(a + 2) * CY] = jnp.concatenate(parts, axis=1) * SL[:, a * CY:a * CY + CY]
    for a in range(CX):
        SL[:, a * CY:a * CY + CY] = smooth(D, a)
    save_g = pltpu.make_async_copy(SL, g_out, local_sem.at[6])
    save_g.start()
    save_h.wait()
    save_e.wait()
    save_g.wait()


def solution(mesh):
    n_gx, n_gy = mesh.shape["gx"], mesh.shape["gy"]
    n_slots = n_gx * CAP
    placed = (
        P(None, None, "gx", "gy"),
        P(None, None, "gx", "gy"),
        P(None, None, "gx", "gy"),
        P("gx", "gy"),
        P(None, "gy"),
        P(),
        P(),
    )
    field = (3, NZ, CX, CY)
    padded = (3, NZ + 1, CX, CY)

    def body(e_field, h_field, target, density, region_list, source_cells, source_amp):
        any_spec = pl.BlockSpec(memory_space=pl.ANY)
        vmem = pl.BlockSpec(memory_space=pltpu.VMEM)

        def run(*refs):
            kernel(n_gx, n_gy, *refs)

        dma = pltpu.SemaphoreType.DMA
        return pl.pallas_call(
            run,
            name="yee_adjoint",
            out_shape=(
                jax.ShapeDtypeStruct(field, F32),
                jax.ShapeDtypeStruct(field, F32),
                jax.ShapeDtypeStruct((NZ, WIDTH), F32),
            ),
            in_specs=[vmem, vmem, vmem, any_spec, any_spec, any_spec, any_spec],
            out_specs=(any_spec, any_spec, any_spec),
            scratch_shapes=[
                pltpu.VMEM(padded, F32),
                pltpu.VMEM(field, F32),
                pltpu.VMEM(field, F32),
                pltpu.VMEM((NZ, WIDTH + 2 * CY), F32),
                pltpu.VMEM((NZ, WIDTH), F32),
                pltpu.VMEM(field, F32),
                pltpu.VMEM(padded, F32),
                pltpu.VMEM((STEPS * 3, NZ, CX, CY), F32),
                pltpu.VMEM((NZ * CX, NSRC), jnp.bfloat16),
                pltpu.VMEM((2 * NZ, CX, 128), F32),
                pltpu.VMEM((NZ, CX, CY), F32),
                pltpu.VMEM((NZ, CX, CY), F32),
                pltpu.VMEM((n_slots, CX, CY), F32),
                pltpu.VMEM((n_slots, CX, CY), F32),
                pltpu.VMEM((n_slots, CX, CY), F32),
                pltpu.VMEM((n_slots, CX, CY), F32),
                pltpu.VMEM((3, 2 * NZ, CY), F32),
                pltpu.VMEM((3, 2 * NZ, CY), F32),
                pltpu.VMEM((3, 5 * NZ, CY), F32),
                pltpu.VMEM((3, 5 * NZ, CY), F32),
                pltpu.VMEM((3, CX, 128), F32),
                pltpu.VMEM((3, CX, 128), F32),
                pltpu.VMEM((3, CX, 128), F32),
                pltpu.VMEM((3, CX, 128), F32),
                pltpu.VMEM((3, NZ, 128), F32),
                pltpu.VMEM((3, 8, 128), F32),
                pltpu.VMEM((2 * NZ, CY), F32),
                pltpu.VMEM((8, 256), jnp.int32),
                pltpu.SMEM((8, 256), jnp.int32),
                dma((8,)),
                dma((2, n_gx)),
                dma((2, n_gx)),
                dma((3, 6)),
                dma((3, 6)),
            ],
            compiler_params=pltpu.CompilerParams(collective_id=0, has_side_effects=True),
        )(region_list.T, source_cells, jnp.swapaxes(source_amp, 0, 1), e_field, h_field, target, density)

    return jax.shard_map(
        body,
        mesh=mesh,
        in_specs=placed,
        out_specs=(P(None, None, "gx", "gy"), P(None, None, "gx", "gy"), P("gx", "gy")),
        check_vma=False,
    )
```
